32 devices in a mesh: section: 8 (over y, x, core), tensor: 4 (over z).
Axes of the slice: x: 2, y: 2, z: 4, core: 2. Of those that a mesh axis runs over, the one named last changes fastest.
Arguments:
- states: bfloat16 [4096, 8192], P('section', 'tensor'), may hold values from -6 to 6
- lengths: int32 [8, 16], P('section'), may hold values from 1 to 96, 512 in all within a row
- routes: int32 [4096, 1], P('section'), may hold values from 0 to 7; in each aligned block of 512 rows (0 to 511, 512 to 1023, ...) at most 128 rows name the same one
- score_gain: float32 [8, 8192], P('section'), may hold values from 0.25 to 1.75
- score_weight: bfloat16 [8, 8192, 4096], P('section', None, 'tensor'), may hold values from -0.0625 to 0.0625
- score_heads: float32 [8, 4096, 2], P('section', 'tensor'), may hold values from -0.09375 to 0.09375
- actor_gain: float32 [8192], replicated, may hold values from 0.25 to 1.75
- actor_weight: bfloat16 [8192, 4096], P(None, 'tensor'), may hold values from -0.0625 to 0.0625
- actor_heads: float32 [4096], P('tensor'), may hold values from -0.09375 to 0.09375
Outputs:
- packed_scores: float32 [2, 8192], P(None, 'section')
- advantages: float32 [4096], P('section')
- actor_grad: float32 [8192, 4096], P('section', 'tensor')
The draws below stay inside these ranges and needn't reach their ends.
Inputs may be any that keep to these rules, and one draw needn't show every extreme that they name: `lengths`: each row sums to 512; its largest entry is exactly 96. `routes`: in the rows of one section (aligned blocks of 512 rows) no member is named by more than 128 rows; some member is named by exactly 128 rows of some block.
All inputs are finite; a program needn't handle non-finite values.
Results may differ from the reference program's by a relative error of at most 0.0055.
Values may be sent and summed in bfloat16 or wider, within the bound.
A program may use at most 128 MiB of HBM per device.

```python
import math
import jax
import jax.numpy as jnp
import numpy as np
from jax import lax

D = 8192
HID = 4096
TOK_SEC = 512
RESP_SEC = 16
LEN_MAX = 96
CAP = 128
SLOTS = 1024
TOKENS = 4096
N_SECTION = 8


def level_of(key, extent, shards, low, top_value):
    gain = 1.0
    for dim, parts in shards:
        steps = jax.random.uniform(jax.random.fold_in(jax.random.fold_in(key, 6), dim), (parts,), jnp.float32, low / len(shards), top_value / len(shards))
        gain = gain * jnp.repeat(jnp.exp(steps), extent[dim] // parts).reshape((-1,) + (1,) * (len(extent) - 1 - dim))
    return gain


def split_up(amount, total, bound, lean):
    loads = [(1 << 20) // math.isqrt(standing ** lean) + 1 for standing in range(2, amount + 1)]
    rest, holding = total - bound - (amount - 1), [1] * (amount - 1)
    while rest > 0:
        candidates = [i for i in range(amount - 1) if holding[i] < bound]
        mass, budget = sum([loads[i] for i in candidates]), rest
        for i in candidates:
            extra = min(bound - holding[i], max(1, budget * loads[i] // mass), rest)
            holding[i] = holding[i] + extra
            rest = rest - extra
    return np.array([bound] + holding)


def uneven(stream_key, count, total, limit, skew):
    if count == 2:
        one = jax.random.randint(stream_key, (), max(1, total - limit), min(limit, total - 1) + 1)
        return jnp.stack([one, total - one])
    tallies = jnp.asarray(split_up(count, total, limit, skew), jnp.int32)
    couples = (count - 1) // 2
    giver, receiver = tallies[1:1 + 2 * couples:2], tallies[2:2 + 2 * couples:2]
    margin = jnp.minimum(giver - 1, limit - receiver)
    passed = jax.random.randint(jax.random.fold_in(stream_key, 1), (couples,), 0, 1 << 20) % (margin + 1)
    tallies = tallies.at[1:1 + 2 * couples:2].set(giver - passed).at[2:2 + 2 * couples:2].set(receiver + passed)
    return tallies[jax.random.permutation(jax.random.fold_in(stream_key, 2), count)]


def shared_out(stream_key, own, number, rows, count, top, limit, lean):
    order = jax.random.permutation(stream_key, count)
    crowded, common = shares(count, rows * top, limit, lean, True), shares(count, rows * top, limit, lean, False)
    places = jnp.arange(count)

    def named(sizes, rotation):
        used = int((sizes > 0).sum())
        fixed = max(1, used // 4)
        shifted = fixed + (places - fixed + rotation * (used - fixed)) % max(1, count - fixed)
        return jnp.zeros((count,), jnp.int32).at[order[jnp.where(places < fixed, places, shifted)]].set(jnp.asarray(sizes, jnp.int32))

    sizes = jnp.where(number % 4 == 0, named(crowded, number // 4), named(common, number - number // 4 - 1))
    mixed = jax.random.permutation(jax.random.fold_in(own, 3), count)
    giver, receiver = mixed[0:count // 2 * 2:2], mixed[1:count // 2 * 2:2]
    margin = jnp.minimum(sizes[giver] - 1, limit - sizes[receiver]) // 2
    margin = jnp.where((giver == order[0]) | (receiver == order[0]) | (sizes[receiver] == 0), 0, jnp.maximum(margin, 0))
    shifted = jax.random.randint(jax.random.fold_in(own, 4), (count // 2,), 0, 1 << 20) % (margin + 1)
    sizes = sizes.at[giver].add(-shifted).at[receiver].add(shifted)
    labels = jnp.searchsorted(jnp.cumsum(sizes), jnp.arange(rows * top), side="right").astype(jnp.int32)
    grid = labels.reshape(top, rows).T
    grid = grid[jax.random.permutation(jax.random.fold_in(own, 1), rows)]
    rotation = jax.random.randint(jax.random.fold_in(own, 2), (rows, 1), 0, top)
    return jnp.take_along_axis(grid, (jnp.arange(top)[None, :] + rotation) % top, axis=1)


def shares(count, total, limit, slope, full):
    loads = [(1 << 20) // math.isqrt(standing ** slope) + 1 for standing in range(1, count + 1)]
    largest = limit if full else min(limit, max(-(-total // count), total * loads[0] // sum(loads)))
    least = 1 if total - largest >= count - 1 else 0
    counts, spare = [largest] + [least] * (count - 1), total - largest - least * (count - 1)
    while spare > 0:
        candidates = [i for i in range(1, count) if counts[i] < largest] or [i for i in range(1, count) if counts[i] < limit]
        mass, budget = sum([loads[i] for i in candidates]), spare
        for i in candidates:
            extra = min(limit - counts[i], max(1, budget * loads[i] // mass), spare)
            counts[i] = counts[i] + extra
            spare = spare - extra
    return np.array(counts)


def normal_values(rng, shape, scale, limit, pieces=(), held_as=jnp.bfloat16):
    array = scale * jax.random.normal(rng, shape, jnp.float32)
    if pieces:
        array = array * level_of(rng, shape, pieces, -0.22, 0.18)
    return jnp.clip(array, -limit, limit).astype(held_as)


def setup_inputs(seed: int = 0) -> dict:
    splits = jax.random.split(jax.random.key(seed), 10)
    states = normal_values(splits[0], (TOKENS, D), 1.0, 6.0, ((0, 8), (1, 4)))
    lengths = jax.vmap(lambda own: uneven(own, RESP_SEC, TOK_SEC, LEN_MAX, 2))(jax.random.split(splits[1], N_SECTION)).reshape((N_SECTION, RESP_SEC)).astype(jnp.int32)
    routes_keys = jax.random.split(jax.random.fold_in(splits[2], 1), TOKENS // TOK_SEC)
    routes_turns = jax.random.permutation(jax.random.fold_in(splits[2], 3), TOKENS // TOK_SEC)
    routes = jax.vmap(lambda own, number: shared_out(jax.random.fold_in(splits[2], 2), own, number, TOK_SEC, N_SECTION, 1, CAP, 2))(routes_keys, routes_turns).reshape((TOKENS, 1))
    score_gain = jnp.clip(1.0 + 0.15 * jax.random.normal(splits[3], (N_SECTION, D), jnp.float32), 0.25, 1.75)
    score_weight = normal_values(splits[4], (N_SECTION, D, HID), D ** -0.5, 0.0625, ((0, 8), (2, 4)))
    score_heads = normal_values(splits[5], (N_SECTION, HID, 2), HID ** -0.5, 0.09375, ((0, 8), (1, 4)), jnp.float32)
    actor_gain = jnp.clip(1.0 + 0.15 * jax.random.normal(splits[6], (D,), jnp.float32), 0.25, 1.75)
    actor_weight = normal_values(splits[7], (D, HID), D ** -0.5, 0.0625, ((1, 4),))
    actor_heads = normal_values(splits[8], (HID,), HID ** -0.5, 0.09375, ((0, 4),), jnp.float32)
    return {"states": states, "lengths": lengths, "routes": routes, "score_gain": score_gain, "score_weight": score_weight, "score_heads": score_heads, "actor_gain": actor_gain, "actor_weight": actor_weight, "actor_heads": actor_heads}


epsilon = 1e-05
trace_decay = 0.95
penalty = 0.1

def compose(earlier, later):
    return (earlier[0] * later[0], later[1] + later[0] * earlier[1])

def advantage_rows(values, rewards, lengths):
    ends = jnp.cumsum(lengths, axis=1) - 1
    steps_idx = jnp.arange(values.shape[1], dtype=jnp.int32)
    last = jnp.any(steps_idx[None, :, None] == ends[:, None, :], axis=2)
    following = jnp.concatenate([values[:, 1:], jnp.zeros_like(values[:, :1])], axis=1)
    delta = jnp.where(last, rewards, following) - values
    weight = jnp.where(last, 0.0, trace_decay).astype(values.dtype)
    carried = lax.associative_scan(compose, (weight[:, ::-1], delta[:, ::-1]), axis=1)
    return carried[1][:, ::-1]

def reference(states, lengths, routes, score_gain, score_weight, score_heads, actor_gain, actor_weight, actor_heads):
    target = routes[:, 0].astype(jnp.int32)
    source = (jnp.arange(TOKENS, dtype=jnp.int32) // TOK_SEC).astype(jnp.int32)
    onehot = (target[:, None] == jnp.arange(N_SECTION, dtype=jnp.int32)[None, :]).astype(jnp.int32)
    blocked = onehot.reshape(N_SECTION, TOK_SEC, N_SECTION)
    before = (jnp.cumsum(blocked, axis=1) - blocked).reshape(TOKENS, N_SECTION)
    placed = lax.optimization_barrier(jnp.sum(before * onehot, axis=1)).astype(jnp.int32)
    slot_index = (source * CAP + placed).astype(jnp.int32)
    packed = jnp.zeros((N_SECTION, SLOTS, D), jnp.bfloat16).at[target, slot_index].set(states)

    def member(member_args):
        row_block, gain_row, member_weight, head_cols = member_args
        widened = row_block.astype(jnp.float32)
        member_scale = lax.rsqrt(lax.optimization_barrier(jnp.mean(widened * widened, axis=1)) + epsilon)
        scaled = (widened * gain_row[None, :]).astype(jnp.bfloat16)
        preact = jnp.dot(scaled, member_weight, preferred_element_type=jnp.float32) * member_scale[:, None]
        return jnp.dot(jax.nn.silu(preact), head_cols, precision=lax.Precision.HIGHEST)
    scored = lax.map(member, (packed, score_gain, score_weight, score_heads))
    packed_scores = jnp.transpose(scored, (2, 0, 1)).reshape(2, N_SECTION * SLOTS)
    token_scores = scored[target, slot_index]
    values = token_scores[:, 0].reshape(N_SECTION, TOK_SEC)
    rewards = token_scores[:, 1].reshape(N_SECTION, TOK_SEC)
    raw_adv = advantage_rows(values, rewards, lengths)
    center = jnp.sum(raw_adv) / TOKENS
    spread = jnp.sum(raw_adv * raw_adv) / TOKENS - center * center
    advantages = ((raw_adv - center) * lax.rsqrt(spread + epsilon)).reshape(TOKENS)
    widened = states.astype(jnp.float32)
    actor_scale = lax.rsqrt(lax.optimization_barrier(jnp.mean(widened * widened, axis=1)) + epsilon)
    gained = (widened * actor_gain[None, :]).astype(jnp.bfloat16)
    actor_pre = jnp.dot(gained, actor_weight, preferred_element_type=jnp.float32) * actor_scale[:, None]
    log_shift = jnp.dot(jax.nn.silu(actor_pre), actor_heads, precision=lax.Precision.HIGHEST)
    ratios = jnp.exp(log_shift)
    logit_slope = penalty * (ratios - 1.0) - ratios * advantages
    sigmoid_pre = jax.nn.sigmoid(actor_pre)
    silu_slope = sigmoid_pre * (1.0 + actor_pre * (1.0 - sigmoid_pre))
    grad_pre = ((logit_slope * actor_scale)[:, None] * actor_heads[None, :] * silu_slope).astype(jnp.bfloat16)
    actor_grad = jnp.dot(gained.T, grad_pre, preferred_element_type=jnp.float32)
    return (packed_scores, advantages, actor_grad)
```

```python
import functools
import jax
import jax.numpy as jnp
from jax import lax
from jax.experimental import pallas as pl
from jax.experimental.pallas import tpu as pltpu
from jax.sharding import PartitionSpec as P

epsilon = 1e-05
trace_decay = 0.95
penalty = 0.1
MESH = pl.DeviceIdType.MESH


def exchange(
    sections, tensors, cap,
    states, dispatch, gain_m, gain_a, weight_m, weight_a,
    acc_m, acc_a, sq_m, sq_a, blocks,
    feats, outbox, inbox, work, wbuf_m, wbuf_a,
    z_send, z_recv, m_send, m_recv, b_send, b_recv, loc_sem, w_sem,
):
    s = lax.axis_index("section")
    t = lax.axis_index("tensor")
    tok, fs = states.shape
    slots = sections * cap
    bps = sections // tensors
    bw = fs // bps
    hid = acc_m.shape[1]
    nt = min(hid, 256)
    chunks = 2
    half = tok // chunks
    up_ok = t + 1 < tensors
    dn_ok = t > 0

    load = pltpu.make_async_copy(states, feats.at[t], loc_sem.at[0])
    load.start()

    barrier = pltpu.get_barrier_semaphore()

    def greet(r, c):
        pl.semaphore_signal(barrier, inc=1, device_id=(lax.rem(s + r, sections), t), device_id_type=MESH)
        return c

    lax.fori_loop(1, sections, greet, 0)

    @pl.when(up_ok)
    def _():
        pl.semaphore_signal(barrier, inc=1, device_id=(s, t + 1), device_id_type=MESH)

    @pl.when(dn_ok)
    def _():
        pl.semaphore_signal(barrier, inc=1, device_id=(s, t - 1), device_id_type=MESH)

    peers = sections - 1 + jnp.where(up_ok, 1, 0) + jnp.where(dn_ok, 1, 0)
    pl.semaphore_wait(barrier, peers)

    acc_m[...] = jnp.zeros_like(acc_m)
    acc_a[...] = jnp.zeros_like(acc_a)
    sq_m[...] = jnp.zeros_like(sq_m)
    sq_a[...] = jnp.zeros_like(sq_a)
    load.wait()

    def z_copy(way, hop, c, shard, dest):
        rows = pl.ds(c * half, half)
        return pltpu.make_async_remote_copy(
            src_ref=feats.at[shard, rows], dst_ref=feats.at[shard, rows],
            send_sem=z_send.at[way, hop, c], recv_sem=z_recv.at[way, hop, c],
            device_id=(s, dest), device_id_type=MESH,
        )

    def m_copy(k, dest, src):
        return pltpu.make_async_remote_copy(
            src_ref=outbox.at[k, pl.ds(pl.multiple_of(dest * cap, cap), cap)],
            dst_ref=inbox.at[k, pl.ds(pl.multiple_of(src * cap, cap), cap)],
            send_sem=m_send.at[k, dest], recv_sem=m_recv.at[k, src],
            device_id=(dest, t), device_id_type=MESH,
        )

    def b_src(dest):
        return feats.at[dest // bps, :, pl.ds(pl.multiple_of(lax.rem(dest, bps) * bw, bw), bw)]

    def b_copy(dest, src):
        return pltpu.make_async_remote_copy(
            src_ref=b_src(dest), dst_ref=blocks.at[src],
            send_sem=b_send.at[dest], recv_sem=b_recv.at[src],
            device_id=(dest, t), device_id_type=MESH,
        )

    def own_copy(k):
        rows = pl.ds(pl.multiple_of(s * cap, cap), cap)
        return pltpu.make_async_copy(outbox.at[k, rows], inbox.at[k, rows], m_recv.at[k, s])

    def w_copy(weight, buf, which, k):
        return pltpu.make_async_copy(
            weight.at[pl.ds(pl.multiple_of(k * fs, fs), fs)], buf, w_sem.at[which]
        )

    rb = 64

    def scale_rows(read, write, sq, gain, rows):
        def step(i, c):
            rr = pl.ds(pl.multiple_of(i * rb, rb), rb)
            x = read(rr).astype(jnp.float32)
            part = x * x
            total = part[:, 0:128]
            for j in range(1, fs // 128):
                total = total + part[:, j * 128:(j + 1) * 128]
            sq[rr, :] += total
            write(rr, (x * gain).astype(jnp.bfloat16))
            return c
        lax.fori_loop(0, rows // rb, step, 0)

    def accumulate(acc, left, buf):
        def step(n, c):
            cols = pl.ds(pl.multiple_of(n * nt, nt), nt)
            acc[:, cols] += jnp.dot(left[...], buf[:, cols], preferred_element_type=jnp.float32)
            return c
        lax.fori_loop(0, hid // nt, step, 0)

    def arrive(hop):
        for c in range(chunks):
            for way in range(2):
                k = t - hop if way == 0 else t + hop
                here = k >= 0 if way == 0 else k < tensors
                onward = up_ok if way == 0 else dn_ok
                dest = t + 1 if way == 0 else t - 1

                @pl.when(jnp.logical_and(hop > 0, here))
                def _():
                    z_copy(way, hop, c, k, t).wait_recv()

                @pl.when(jnp.logical_and(here, onward))
                def _():
                    z_copy(way, hop + 1, c, k, dest).start()

    def process(k):
        w_copy(weight_a, wbuf_a, 0, k).start()
        pt = min(fs, 256)

        def pack(n, c):
            cols = pl.ds(pl.multiple_of(n * pt, pt), pt)
            outbox[k, :, cols] = jnp.dot(
                dispatch[...], feats[k, :, cols], preferred_element_type=jnp.float32
            ).astype(jnp.bfloat16)
            return c

        lax.fori_loop(0, fs // pt, pack, 0)
        own_copy(k).start()

        def send(r, c):
            m_copy(k, lax.rem(s + r, sections), s).start()
            return c

        lax.fori_loop(1, sections, send, 0)

    def actor(k):
        gain = gain_a[k]

        def write(rr, v):
            work[rr, :] = v

        scale_rows(lambda rr: feats[k, rr, :], write, sq_a, gain, tok)
        w_copy(weight_a, wbuf_a, 0, k).wait()
        accumulate(acc_a, work, wbuf_a)

    def member(k):
        w_copy(weight_m, wbuf_m, 1, k).start()
        own_copy(k).wait()

        def take(r, c):
            m_copy(k, s, lax.rem(s + r, sections)).wait_recv()
            return c

        lax.fori_loop(1, sections, take, 0)
        gain = gain_m[k]

        def write(rr, v):
            inbox[k, rr, :] = v

        scale_rows(lambda rr: inbox[k, rr, :], write, sq_m, gain, slots)
        w_copy(weight_m, wbuf_m, 1, k).wait()
        accumulate(acc_m, inbox.at[k], wbuf_m)

    def hop_body(hop, c):
        @pl.when(hop < tensors)
        def _():
            arrive(hop)

        def inner(way, c):
            k = jnp.where(way == 0, t - hop, t + hop)
            fine = jnp.logical_and(jnp.logical_and(k >= 0, k < tensors), jnp.logical_or(hop > 0, way == 0))
            fine = jnp.logical_and(fine, hop < tensors)

            @pl.when(fine)
            def _():
                process(k)
                actor(k)
            return c

        lax.fori_loop(0, 2, inner, 0)

        @pl.when(hop == tensors - 1)
        def _():
            pltpu.make_async_copy(b_src(s), blocks.at[s], b_recv.at[s]).start()

            def send(r, c):
                b_copy(lax.rem(s + r, sections), s).start()
                return c

            lax.fori_loop(1, sections, send, 0)

        def inner_m(way, c):
            k = jnp.where(way == 0, t - (hop - 1), t + (hop - 1))
            fine = jnp.logical_and(jnp.logical_and(k >= 0, k < tensors), jnp.logical_or(hop > 1, way == 0))
            fine = jnp.logical_and(fine, hop > 0)

            @pl.when(fine)
            def _():
                member(k)
            return c

        lax.fori_loop(0, 2, inner_m, 0)
        return c

    lax.fori_loop(0, tensors + 1, hop_body, 0)

    pltpu.make_async_copy(b_src(s), blocks.at[s], b_recv.at[s]).wait()

    def finish(r, c):
        other = lax.rem(s + r, sections)
        b_copy(s, other).wait_recv()
        b_copy(other, s).wait_send()

        def sent(k, c):
            m_copy(k, other, s).wait_send()
            return c

        return lax.fori_loop(0, tensors, sent, c)

    lax.fori_loop(1, sections, finish, 0)

    def drain(hop, c):
        for cc in range(chunks):
            @pl.when(jnp.logical_and(t - hop >= 0, up_ok))
            def _():
                z_copy(0, hop + 1, cc, t - hop, t + 1).wait_send()

            @pl.when(jnp.logical_and(t + hop < tensors, dn_ok))
            def _():
                z_copy(1, hop + 1, cc, t + hop, t - 1).wait_send()
        return c

    lax.fori_loop(0, tensors, drain, 0)


def body(
    states, lengths, routes, score_gain, score_weight, score_heads,
    actor_gain, actor_weight, actor_heads,
):
    sections = lax.axis_size("section")
    tensors = lax.axis_size("tensor")
    tok, fs = states.shape
    cap = 2 * tok // sections
    slots = sections * cap
    width = score_gain.shape[1]
    hid = actor_weight.shape[1]
    bw = width // sections
    target = routes[:, 0]
    ids = jnp.arange(tok, dtype=jnp.int32)
    same = jnp.logical_and(target[:, None] == target[None, :], ids[:, None] > ids[None, :])
    placed = jnp.sum(same.astype(jnp.int32), axis=1)
    slot_index = target * cap + placed
    hit = jnp.arange(slots, dtype=jnp.int32)[:, None] == slot_index[None, :]
    dispatch = hit.astype(jnp.bfloat16)

    vmem = pl.BlockSpec(memory_space=pltpu.VMEM)
    any_ = pl.BlockSpec(memory_space=pl.ANY)
    f32, bf16 = jnp.float32, jnp.bfloat16
    acc_m, acc_a, sq_m, sq_a, blocks = pl.pallas_call(
        functools.partial(exchange, sections, tensors, cap),
        out_shape=(
            jax.ShapeDtypeStruct((slots, hid), f32),
            jax.ShapeDtypeStruct((tok, hid), f32),
            jax.ShapeDtypeStruct((slots, 128), f32),
            jax.ShapeDtypeStruct((tok, 128), f32),
            jax.ShapeDtypeStruct((sections, tok, bw), bf16),
        ),
        in_specs=[any_, vmem, vmem, vmem, any_, any_],
        out_specs=(vmem, vmem, vmem, vmem, any_),
        scratch_shapes=[
            pltpu.VMEM((tensors, tok, fs), bf16),
            pltpu.VMEM((tensors, slots, fs), bf16),
            pltpu.VMEM((tensors, slots, fs), bf16),
            pltpu.VMEM((tok, fs), bf16),
            pltpu.VMEM((fs, hid), bf16),
            pltpu.VMEM((fs, hid), bf16),
            pltpu.SemaphoreType.DMA((2, tensors + 1, 2)),
            pltpu.SemaphoreType.DMA((2, tensors + 1, 2)),
            pltpu.SemaphoreType.DMA((tensors, sections)),
            pltpu.SemaphoreType.DMA((tensors, sections)),
            pltpu.SemaphoreType.DMA((sections,)),
            pltpu.SemaphoreType.DMA((sections,)),
            pltpu.SemaphoreType.DMA((1,)),
            pltpu.SemaphoreType.DMA((2,)),
        ],
        compiler_params=pltpu.CompilerParams(
            collective_id=0, has_side_effects=True, vmem_limit_bytes=67043328
        ),
    )(
        states, dispatch, score_gain[0].reshape(tensors, 1, fs),
        actor_gain.reshape(tensors, 1, fs), score_weight[0], actor_weight,
    )

    actor_scale = lax.rsqrt(jnp.sum(sq_a, axis=1) / width + epsilon)
    actor_pre = acc_a * actor_scale[:, None]
    sigmoid_pre = jax.nn.sigmoid(actor_pre)
    silu_slope = sigmoid_pre * (1.0 + actor_pre * (1.0 - sigmoid_pre))
    early = (actor_scale[:, None] * actor_heads[None, :] * silu_slope).astype(bf16)
    every_early = lax.all_gather(early, "section", axis=0, tiled=True)
    shift_part = jnp.sum(actor_pre * sigmoid_pre * actor_heads[None, :], axis=1)

    member_scale = lax.rsqrt(jnp.sum(sq_m, axis=1) / width + epsilon)
    preact = acc_m * member_scale[:, None]
    act = jax.nn.silu(preact)
    heads = score_heads[0]
    parts = jnp.stack(
        [jnp.sum(act * heads[:, 0][None, :], axis=1), jnp.sum(act * heads[:, 1][None, :], axis=1)]
    )
    scores, log_shift = lax.psum((parts, shift_part), "tensor")
    returned = lax.all_to_all(
        scores.reshape(2, sections, cap), "section", split_axis=1, concat_axis=1, tiled=True
    ).reshape(2, slots)
    values = jnp.sum(jnp.where(hit, returned[0][:, None], 0.0), axis=0)
    rewards = jnp.sum(jnp.where(hit, returned[1][:, None], 0.0), axis=0)

    ends = jnp.sum(
        jnp.where(jnp.arange(lengths.shape[1])[:, None] <= jnp.arange(lengths.shape[1])[None, :],
                  lengths[0][:, None], 0), axis=0) - 1
    last = jnp.any(ids[:, None] == ends[None, :], axis=1)
    response = jnp.sum((ids[:, None] > ends[None, :]).astype(jnp.int32), axis=1)
    gap = ids[None, :] - ids[:, None]
    linked = jnp.logical_and(gap >= 0, response[:, None] == response[None, :])
    decay = jnp.where(linked, jnp.exp(gap.astype(f32) * jnp.log(f32(trace_decay))), 0.0)
    following = jnp.concatenate([values[1:], jnp.zeros_like(values[:1])])
    delta = jnp.where(last, rewards, following) - values
    raw = jnp.sum(decay * delta[None, :], axis=1)

    both = lax.all_gather(jnp.stack([raw, log_shift]), "section", axis=0)
    raw_all = both[:, 0].reshape(-1)
    shift_all = both[:, 1].reshape(-1)
    total = tok * sections
    center = jnp.sum(raw_all) / total
    spread = jnp.sum(raw_all * raw_all) / total - center * center
    inv = lax.rsqrt(spread + epsilon)
    advantages = (raw - center) * inv
    ratios = jnp.exp(shift_all)
    slope = penalty * (ratios - 1.0) - ratios * ((raw_all - center) * inv)

    gain_own = lax.dynamic_slice(actor_gain, (lax.axis_index("section") * bw,), (bw,))
    left = (blocks.reshape(total, bw).astype(f32) * gain_own[None, :]).astype(bf16)
    right = (every_early.astype(f32) * slope[:, None]).astype(bf16)
    actor_grad = lax.dot_general(
        left, right, (((0,), (0,)), ((), ())), preferred_element_type=f32
    )
    return (scores, advantages, actor_grad)


def solution(mesh):
    in_specs = (
        P("section", "tensor"),
        P("section", None),
        P("section", None),
        P("section", None),
        P("section", None, "tensor"),
        P("section", "tensor", None),
        P(),
        P(None, "tensor"),
        P("tensor"),
    )
    out_specs = (P(None, "section"), P("section"), P("section", "tensor"))
    return jax.shard_map(body, mesh=mesh, in_specs=in_specs, out_specs=out_specs, check_vma=False)
```

```python
import functools
import jax
import jax.numpy as jnp
from jax import lax
from jax.experimental import pallas as pl
from jax.experimental.pallas import tpu as pltpu
from jax.sharding import PartitionSpec as P

epsilon = 1e-05
trace_decay = 0.95
penalty = 0.1
MESH = pl.DeviceIdType.MESH


def exchange(
    sections, tensors, cap,
    states, dispatch, gain_m, gain_a, weight_m, weight_a, heads_m, heads_a, final,
    scores, pairs, blocks, hidden,
    acc_m, acc_a, sq_m, sq_a, lanes, part, part_a, back, early, feats, outbox, inbox, work, wbuf_m, wbuf_a,
    z_send, z_recv, m_send, m_recv, b_send, b_recv, loc_sem, w_sem,
    t_send, t_recv, u_send, u_recv, r_send, r_recv, p_send, p_recv, g_send, g_recv, g_pass,
):
    s = lax.axis_index("section")
    t = lax.axis_index("tensor")
    tok, fs = states.shape
    slots = sections * cap
    bps = sections // tensors
    bw = fs // bps
    hid = acc_m.shape[1]
    nt = min(hid, 256)
    chunks = 2
    half = tok // chunks
    up_ok = t + 1 < tensors
    dn_ok = t > 0

    load = pltpu.make_async_copy(states, feats.at[t], loc_sem.at[0])
    load.start()

    barrier = pltpu.get_barrier_semaphore()

    def greet(r, c):
        pl.semaphore_signal(barrier, inc=1, device_id=(lax.rem(s + r, sections), t), device_id_type=MESH)
        return c

    lax.fori_loop(1, sections, greet, 0)

    def greet_z(r, c):
        pl.semaphore_signal(barrier, inc=1, device_id=(s, lax.rem(t + r, tensors)), device_id_type=MESH)
        return c

    lax.fori_loop(1, tensors, greet_z, 0)
    pl.semaphore_wait(barrier, sections - 1 + tensors - 1)

    acc_m[...] = jnp.zeros_like(acc_m)
    acc_a[...] = jnp.zeros_like(acc_a)
    sq_m[...] = jnp.zeros_like(sq_m)
    sq_a[...] = jnp.zeros_like(sq_a)
    load.wait()

    def z_copy(way, hop, c, shard, dest):
        rows = pl.ds(c * half, half)
        return pltpu.make_async_remote_copy(
            src_ref=feats.at[shard, rows], dst_ref=feats.at[shard, rows],
            send_sem=z_send.at[way, hop, c], recv_sem=z_recv.at[way, hop, c],
            device_id=(s, dest), device_id_type=MESH,
        )

    def m_copy(k, dest, src):
        return pltpu.make_async_remote_copy(
            src_ref=outbox.at[k, pl.ds(pl.multiple_of(dest * cap, cap), cap)],
            dst_ref=inbox.at[k, pl.ds(pl.multiple_of(src * cap, cap), cap)],
            send_sem=m_send.at[k, dest], recv_sem=m_recv.at[k, src],
            device_id=(dest, t), device_id_type=MESH,
        )

    def b_src(dest):
        return feats.at[dest // bps, :, pl.ds(pl.multiple_of(lax.rem(dest, bps) * bw, bw), bw)]

    def b_copy(dest, src):
        return pltpu.make_async_remote_copy(
            src_ref=b_src(dest), dst_ref=blocks.at[src],
            send_sem=b_send.at[dest], recv_sem=b_recv.at[src],
            device_id=(dest, t), device_id_type=MESH,
        )

    def own_copy(k):
        rows = pl.ds(pl.multiple_of(s * cap, cap), cap)
        return pltpu.make_async_copy(outbox.at[k, rows], inbox.at[k, rows], m_recv.at[k, s])

    def w_copy(weight, buf, which, k):
        return pltpu.make_async_copy(
            weight.at[pl.ds(pl.multiple_of(k * fs, fs), fs)], buf, w_sem.at[which]
        )

    rb = 64

    def scale_rows(read, write, sq, gain, rows):
        def step(i, c):
            rr = pl.ds(pl.multiple_of(i * rb, rb), rb)
            x = read(rr).astype(jnp.float32)
            part = x * x
            total = part[:, 0:128]
            for j in range(1, fs // 128):
                total = total + part[:, j * 128:(j + 1) * 128]
            sq[rr, :] += total
            write(rr, (x * gain).astype(jnp.bfloat16))
            return c
        lax.fori_loop(0, rows // rb, step, 0)

    def accumulate(acc, left, buf):
        def step(n, c):
            cols = pl.ds(pl.multiple_of(n * nt, nt), nt)
            acc[:, cols] += jnp.dot(left[...], buf[:, cols], preferred_element_type=jnp.float32)
            return c
        lax.fori_loop(0, hid // nt, step, 0)

    def arrive(hop):
        for c in range(chunks):
            for way in range(2):
                k = t - hop if way == 0 else t + hop
                here = k >= 0 if way == 0 else k < tensors
                onward = up_ok if way == 0 else dn_ok
                dest = t + 1 if way == 0 else t - 1

                @pl.when(jnp.logical_and(hop > 0, here))
                def _():
                    z_copy(way, hop, c, k, t).wait_recv()

                @pl.when(jnp.logical_and(here, onward))
                def _():
                    z_copy(way, hop + 1, c, k, dest).start()

    def process(k):
        w_copy(weight_a, wbuf_a, 0, k).start()
        pt = min(fs, 256)

        def pack(n, c):
            cols = pl.ds(pl.multiple_of(n * pt, pt), pt)
            outbox[k, :, cols] = jnp.dot(
                dispatch[...], feats[k, :, cols], preferred_element_type=jnp.float32
            ).astype(jnp.bfloat16)
            return c

        lax.fori_loop(0, fs // pt, pack, 0)
        own_copy(k).start()

        def send(r, c):
            m_copy(k, lax.rem(s + r, sections), s).start()
            return c

        lax.fori_loop(1, sections, send, 0)

    def actor(k):
        gain = gain_a[k]

        def write(rr, v):
            work[rr, :] = v

        scale_rows(lambda rr: feats[k, rr, :], write, sq_a, gain, tok)
        w_copy(weight_a, wbuf_a, 0, k).wait()
        accumulate(acc_a, work, wbuf_a)

    def member(k):
        w_copy(weight_m, wbuf_m, 1, k).start()
        own_copy(k).wait()

        def take(r, c):
            m_copy(k, s, lax.rem(s + r, sections)).wait_recv()
            return c

        lax.fori_loop(1, sections, take, 0)
        gain = gain_m[k]

        def write(rr, v):
            inbox[k, rr, :] = v

        scale_rows(lambda rr: inbox[k, rr, :], write, sq_m, gain, slots)
        w_copy(weight_m, wbuf_m, 1, k).wait()
        accumulate(acc_m, inbox.at[k], wbuf_m)

    partner = s + 1 - 2 * lax.rem(s, 2)
    chips = sections // 2
    width = fs * tensors

    def send_block(r, c):
        b_copy(lax.rem(s + r, sections), s).start()
        return c

    def g_copy(dest, src):
        return pltpu.make_async_remote_copy(
            src_ref=early, dst_ref=hidden.at[src],
            send_sem=g_send.at[dest], recv_sem=g_recv.at[src],
            device_id=(dest, t), device_id_type=MESH,
        )

    def g_relay(src):
        return pltpu.make_async_remote_copy(
            src_ref=hidden.at[src], dst_ref=hidden.at[src],
            send_sem=g_pass.at[src], recv_sem=g_recv.at[src],
            device_id=(partner, t), device_id_type=MESH,
        )

    def own_hidden():
        return pltpu.make_async_copy(early, hidden.at[s], g_recv.at[s])

    def t_copy(dest, src):
        return pltpu.make_async_remote_copy(
            src_ref=part.at[src], dst_ref=part.at[src],
            send_sem=t_send.at[dest], recv_sem=t_recv.at[src],
            device_id=(s, dest), device_id_type=MESH,
        )

    def u_copy(dest, src):
        return pltpu.make_async_remote_copy(
            src_ref=part_a.at[src], dst_ref=part_a.at[src],
            send_sem=u_send.at[dest], recv_sem=u_recv.at[src],
            device_id=(s, dest), device_id_type=MESH,
        )

    def r_copy(dest, src):
        return pltpu.make_async_remote_copy(
            src_ref=scores.at[dest], dst_ref=back.at[src],
            send_sem=r_send.at[dest], recv_sem=r_recv.at[src],
            device_id=(dest, t), device_id_type=MESH,
        )

    def p_copy(dest, src):
        return pltpu.make_async_remote_copy(
            src_ref=pairs.at[src], dst_ref=pairs.at[src],
            send_sem=p_send.at[dest], recv_sem=p_recv.at[src],
            device_id=(dest, t), device_id_type=MESH,
        )

    def across(x):
        return lax.dot_general(
            jnp.ones((8, 128), jnp.float32), x, (((1,), (1,)), ((), ())),
            precision=lax.Precision.HIGHEST, preferred_element_type=jnp.float32,
        )

    def fold(x):
        total = x[:, 0:128]
        for j in range(1, hid // 128):
            total = total + x[:, j * 128:(j + 1) * 128]
        return total

    def hidden_step():
        def step(i, c):
            rr = pl.ds(pl.multiple_of(i * rb, rb), rb)
            scale = lax.rsqrt(jnp.sum(sq_a[rr, :], axis=1, keepdims=True) / width + epsilon)
            pre = acc_a[rr, :] * scale
            sig = 1.0 / (1.0 + jnp.exp(-pre))
            row = heads_a[...]
            early[rr, :] = (scale * row * (sig * (1.0 + pre * (1.0 - sig)))).astype(jnp.bfloat16)
            lanes[0, rr, :] = fold(pre * sig * row)
            return c

        lax.fori_loop(0, tok // rb, step, 0)
        part_a[t] = across(lanes[0, 0:tok, :])

        def send_u(r, c):
            u_copy(lax.rem(t + r, tensors), t).start()
            return c

        lax.fori_loop(1, tensors, send_u, 0)
        own_hidden().start()
        g_copy(partner, s).start()

        def send_g(r, c):
            g_copy(lax.rem(s + 2 * r, sections), s).start()
            return c

        lax.fori_loop(1, chips, send_g, 0)

    def score_step():
        def step(i, c):
            rr = pl.ds(pl.multiple_of(i * rb, rb), rb)
            scale = lax.rsqrt(jnp.sum(sq_m[rr, :], axis=1, keepdims=True) / width + epsilon)
            pre = acc_m[rr, :] * scale
            act = pre * (1.0 / (1.0 + jnp.exp(-pre)))
            lanes[0, rr, :] = fold(act * heads_m[0:1, :])
            lanes[1, rr, :] = fold(act * heads_m[1:2, :])
            return c

        lax.fori_loop(0, slots // rb, step, 0)
        first = lax.broadcasted_iota(jnp.int32, (8, cap), 0) == 0

        def gather(d, c):
            rr = pl.ds(pl.multiple_of(d * cap, cap), cap)
            part[t, d] = jnp.where(first, across(lanes[0, rr, :]), across(lanes[1, rr, :]))
            return c

        lax.fori_loop(0, sections, gather, 0)

        def send_t(r, c):
            t_copy(lax.rem(t + r, tensors), t).start()
            return c

        lax.fori_loop(1, tensors, send_t, 0)

        def take_t(r, c):
            t_copy(t, lax.rem(t + r, tensors)).wait_recv()
            u_copy(t, lax.rem(t + r, tensors)).wait_recv()
            return c

        lax.fori_loop(1, tensors, take_t, 0)
        scores[...] = lax.fori_loop(1, tensors, lambda k, v: v + part[k], part[0])
        shift = lax.fori_loop(1, tensors, lambda k, v: v + part_a[k], part_a[0])

        def send_r(r, c):
            r_copy(lax.rem(s + r, sections), s).start()
            return c

        lax.fori_loop(1, sections, send_r, 0)
        back[s] = scores[s]
        lax.fori_loop(sections - spare, sections, send_block, 0)

        def take_r(r, c):
            r_copy(s, lax.rem(s + r, sections)).wait_recv()
            return c

        lax.fori_loop(1, sections, take_r, 0)

        def pick(m, v):
            x = back[m]
            hi = x.astype(jnp.bfloat16)
            rest = x - hi.astype(jnp.float32)
            mid = rest.astype(jnp.bfloat16)
            low = (rest - mid.astype(jnp.float32)).astype(jnp.bfloat16)
            rows = dispatch[pl.ds(pl.multiple_of(m * cap, cap), cap), :]
            for piece in (low, mid, hi):
                v = v + jnp.dot(piece, rows, preferred_element_type=jnp.float32)
            return v

        picked = lax.fori_loop(0, sections, pick, jnp.zeros((8, tok), jnp.float32))
        values = jnp.broadcast_to(picked[0:1, :], (8, tok))
        rewards = jnp.broadcast_to(picked[1:2, :], (8, tok))
        ended = jnp.broadcast_to(final[...], (8, tok)) > 0.5
        total = jnp.where(ended, rewards, pltpu.roll(values, tok - 1, 1)) - values
        carry = jnp.where(ended, 0.0, trace_decay)
        reach = 1
        while reach < tok:
            total = total + carry * pltpu.roll(total, tok - reach, 1)
            carry = carry * pltpu.roll(carry, tok - reach, 1)
            reach *= 2
        top = lax.broadcasted_iota(jnp.int32, (8, tok), 0) == 0
        pairs[s] = jnp.where(top, total, shift)

        def send_p(r, c):
            p_copy(lax.rem(s + r, sections), s).start()
            return c

        lax.fori_loop(1, sections, send_p, 0)

        def relay(r, c):
            src = lax.rem(s + 2 * r, sections)
            g_copy(s, src).wait_recv()
            g_relay(src).start()
            return c

        lax.fori_loop(1, chips, relay, 0)
        own_hidden().wait()

    def settle():
        g_copy(s, partner).wait_recv()
        g_copy(partner, s).wait_send()

        def done_g(r, c):
            other = lax.rem(s + 2 * r, sections)
            g_copy(other, s).wait_send()
            g_relay(other).wait_send()
            g_copy(s, lax.rem(partner + 2 * r, sections)).wait_recv()
            return c

        lax.fori_loop(1, chips, done_g, 0)

        def done_z(r, c):
            other = lax.rem(t + r, tensors)
            t_copy(other, t).wait_send()
            u_copy(other, t).wait_send()
            return c

        lax.fori_loop(1, tensors, done_z, 0)

        def done_s(r, c):
            other = lax.rem(s + r, sections)
            r_copy(other, s).wait_send()
            p_copy(other, s).wait_send()
            p_copy(s, other).wait_recv()
            return c

        lax.fori_loop(1, sections, done_s, 0)

    spare = max(1, 3 * sections // 8)

    def hop_body(hop, c):
        @pl.when(hop < tensors)
        def _():
            arrive(hop)

        def inner(way, c):
            k = jnp.where(way == 0, t - hop, t + hop)
            fine = jnp.logical_and(jnp.logical_and(k >= 0, k < tensors), jnp.logical_or(hop > 0, way == 0))
            fine = jnp.logical_and(fine, hop < tensors)

            @pl.when(fine)
            def _():
                process(k)
                actor(k)
            return c

        lax.fori_loop(0, 2, inner, 0)

        @pl.when(hop == tensors - 1)
        def _():
            hidden_step()
            pltpu.make_async_copy(b_src(s), blocks.at[s], b_recv.at[s]).start()
            lax.fori_loop(1, sections - spare, send_block, 0)

        def inner_m(way, c):
            k = jnp.where(way == 0, t - (hop - 1), t + (hop - 1))
            fine = jnp.logical_and(jnp.logical_and(k >= 0, k < tensors), jnp.logical_or(hop > 1, way == 0))
            fine = jnp.logical_and(fine, hop > 0)

            @pl.when(fine)
            def _():
                member(k)
            return c

        lax.fori_loop(0, 2, inner_m, 0)
        return c

    lax.fori_loop(0, tensors + 1, hop_body, 0)
    score_step()
    settle()

    pltpu.make_async_copy(b_src(s), blocks.at[s], b_recv.at[s]).wait()

    def finish(r, c):
        other = lax.rem(s + r, sections)
        b_copy(s, other).wait_recv()
        b_copy(other, s).wait_send()

        def sent(k, c):
            m_copy(k, other, s).wait_send()
            return c

        return lax.fori_loop(0, tensors, sent, c)

    lax.fori_loop(1, sections, finish, 0)

    def drain(hop, c):
        for cc in range(chunks):
            @pl.when(jnp.logical_and(t - hop >= 0, up_ok))
            def _():
                z_copy(0, hop + 1, cc, t - hop, t + 1).wait_send()

            @pl.when(jnp.logical_and(t + hop < tensors, dn_ok))
            def _():
                z_copy(1, hop + 1, cc, t + hop, t - 1).wait_send()
        return c

    lax.fori_loop(0, tensors, drain, 0)


def body(
    states, lengths, routes, score_gain, score_weight, score_heads,
    actor_gain, actor_weight, actor_heads,
):
    sections = lax.axis_size("section")
    tensors = lax.axis_size("tensor")
    tok, fs = states.shape
    cap = 2 * tok // sections
    slots = sections * cap
    width = score_gain.shape[1]
    hid = actor_weight.shape[1]
    bw = width // sections
    target = routes[:, 0]
    ids = jnp.arange(tok, dtype=jnp.int32)
    same = jnp.logical_and(target[:, None] == target[None, :], ids[:, None] > ids[None, :])
    placed = jnp.sum(same.astype(jnp.int32), axis=1)
    slot_index = target * cap + placed
    hit = jnp.arange(slots, dtype=jnp.int32)[:, None] == slot_index[None, :]
    dispatch = hit.astype(jnp.bfloat16)
    count = lengths.shape[1]
    order = jnp.arange(count, dtype=jnp.int32)
    ends = jnp.sum(jnp.where(order[:, None] <= order[None, :], lengths[0][:, None], 0), axis=0) - 1
    last = jnp.any(ends[:, None] == ids[None, :], axis=0)

    vmem = pl.BlockSpec(memory_space=pltpu.VMEM)
    any_ = pl.BlockSpec(memory_space=pl.ANY)
    f32, bf16 = jnp.float32, jnp.bfloat16
    scores, pairs, blocks, hidden = pl.pallas_call(
        functools.partial(exchange, sections, tensors, cap),
        out_shape=(
            jax.ShapeDtypeStruct((sections, 8, cap), f32),
            jax.ShapeDtypeStruct((sections, 8, tok), f32),
            jax.ShapeDtypeStruct((sections, tok, bw), bf16),
            jax.ShapeDtypeStruct((sections, tok, hid), bf16),
        ),
        in_specs=[any_, vmem, vmem, vmem, any_, any_, vmem, vmem, vmem],
        out_specs=(vmem, vmem, any_, any_),
        scratch_shapes=[
            pltpu.VMEM((slots, hid), f32),
            pltpu.VMEM((tok, hid), f32),
            pltpu.VMEM((slots, 128), f32),
            pltpu.VMEM((tok, 128), f32),
            pltpu.VMEM((2, max(slots, tok), 128), f32),
            pltpu.VMEM((tensors, sections, 8, cap), f32),
            pltpu.VMEM((tensors, 8, tok), f32),
            pltpu.VMEM((sections, 8, cap), f32),
            pltpu.VMEM((tok, hid), bf16),
            pltpu.VMEM((tensors, tok, fs), bf16),
            pltpu.VMEM((tensors, slots, fs), bf16),
            pltpu.VMEM((tensors, slots, fs), bf16),
            pltpu.VMEM((tok, fs), bf16),
            pltpu.VMEM((fs, hid), bf16),
            pltpu.VMEM((fs, hid), bf16),
            pltpu.SemaphoreType.DMA((2, tensors + 1, 2)),
            pltpu.SemaphoreType.DMA((2, tensors + 1, 2)),
            pltpu.SemaphoreType.DMA((tensors, sections)),
            pltpu.SemaphoreType.DMA((tensors, sections)),
            pltpu.SemaphoreType.DMA((sections,)),
            pltpu.SemaphoreType.DMA((sections,)),
            pltpu.SemaphoreType.DMA((1,)),
            pltpu.SemaphoreType.DMA((2,)),
            pltpu.SemaphoreType.DMA((tensors,)),
            pltpu.SemaphoreType.DMA((tensors,)),
            pltpu.SemaphoreType.DMA((tensors,)),
            pltpu.SemaphoreType.DMA((tensors,)),
            pltpu.SemaphoreType.DMA((sections,)),
            pltpu.SemaphoreType.DMA((sections,)),
            pltpu.SemaphoreType.DMA((sections,)),
            pltpu.SemaphoreType.DMA((sections,)),
            pltpu.SemaphoreType.DMA((sections,)),
            pltpu.SemaphoreType.DMA((sections,)),
            pltpu.SemaphoreType.DMA((sections,)),
        ],
        compiler_params=pltpu.CompilerParams(
            collective_id=0, has_side_effects=True, vmem_limit_bytes=67043328
        ),
    )(
        states, dispatch, score_gain[0].reshape(tensors, 1, fs),
        actor_gain.reshape(tensors, 1, fs), score_weight[0], actor_weight,
        jnp.transpose(score_heads[0]), actor_heads[None, :], last.astype(f32)[None, :],
    )

    raw_all = pairs[:, 0].reshape(-1)
    shift_all = pairs[:, 1].reshape(-1)
    raw = lax.dynamic_index_in_dim(pairs, lax.axis_index("section"), 0, keepdims=False)[0]
    total = tok * sections
    center = jnp.sum(raw_all) / total
    spread = jnp.sum(raw_all * raw_all) / total - center * center
    inv = lax.rsqrt(spread + epsilon)
    advantages = (raw - center) * inv
    ratios = jnp.exp(shift_all)
    slope = penalty * (ratios - 1.0) - ratios * ((raw_all - center) * inv)

    gain_own = lax.dynamic_slice(actor_gain, (lax.axis_index("section") * bw,), (bw,))
    left = (blocks.reshape(total, bw).astype(f32) * gain_own[None, :]).astype(bf16)
    right = (hidden.reshape(total, hid).astype(f32) * slope[:, None]).astype(bf16)
    actor_grad = lax.dot_general(
        left, right, (((0,), (0,)), ((), ())), preferred_element_type=f32
    )
    packed_scores = jnp.transpose(scores[:, :2], (1, 0, 2)).reshape(2, slots)
    return (packed_scores, advantages, actor_grad)


def solution(mesh):
    in_specs = (
        P("section", "tensor"),
        P("section", None),
        P("section", None),
        P("section", None),
        P("section", None, "tensor"),
        P("section", "tensor", None),
        P(),
        P(None, "tensor"),
        P("tensor"),
    )
    out_specs = (P(None, "section"), P("section"), P("section", "tensor"))
    return jax.shard_map(body, mesh=mesh, in_specs=in_specs, out_specs=out_specs, check_vma=False)
```

```python
import functools
import jax
import jax.numpy as jnp
from jax import lax
from jax.experimental import pallas as pl
from jax.experimental.pallas import tpu as pltpu
from jax.sharding import PartitionSpec as P

epsilon = 1e-05
trace_decay = 0.95
penalty = 0.1
MESH = pl.DeviceIdType.MESH


def exchange(
    sections, tensors, cap,
    states, dispatch, gain_m, gain_a, weight_m, weight_a, heads_m, heads_a, final,
    scores, pairs, blocks, hidden,
    acc_m, acc_a, sq_m, sq_a, lanes, part, part_a, back, early, feats, outbox, inbox, work, wbuf_m, wbuf_a,
    z_send, z_recv, m_send, m_recv, b_send, b_recv, loc_sem, w_sem,
    t_send, t_recv, u_send, u_recv, r_send, r_recv, p_send, p_recv, g_send, g_recv, g_pass,
    q_send, q_recv, y_send, y_recv,
):
    s = lax.axis_index("section")
    t = lax.axis_index("tensor")
    tok, fs = states.shape
    slots = sections * cap
    bps = sections // tensors
    bw = fs // bps
    hid = acc_m.shape[1]
    nt = min(hid, 256)
    chunks = 2
    half = tok // chunks
    up_ok = t + 1 < tensors
    dn_ok = t > 0

    load = pltpu.make_async_copy(states, feats.at[t], loc_sem.at[0])
    load.start()

    barrier = pltpu.get_barrier_semaphore()

    def greet(r, c):
        pl.semaphore_signal(barrier, inc=1, device_id=(lax.rem(s + r, sections), t), device_id_type=MESH)
        return c

    lax.fori_loop(1, sections, greet, 0)

    def greet_z(r, c):
        pl.semaphore_signal(barrier, inc=1, device_id=(s, lax.rem(t + r, tensors)), device_id_type=MESH)
        return c

    lax.fori_loop(1, tensors, greet_z, 0)
    pl.semaphore_wait(barrier, sections - 1 + tensors - 1)

    acc_m[...] = jnp.zeros_like(acc_m)
    acc_a[...] = jnp.zeros_like(acc_a)
    sq_m[...] = jnp.zeros_like(sq_m)
    sq_a[...] = jnp.zeros_like(sq_a)
    load.wait()

    def z_copy(way, hop, c, shard, dest):
        rows = pl.ds(c * half, half)
        return pltpu.make_async_remote_copy(
            src_ref=feats.at[shard, rows], dst_ref=feats.at[shard, rows],
            send_sem=z_send.at[way, hop, c], recv_sem=z_recv.at[way, hop, c],
            device_id=(s, dest), device_id_type=MESH,
        )

    def m_copy(k, dest, src):
        return pltpu.make_async_remote_copy(
            src_ref=outbox.at[k, pl.ds(pl.multiple_of(dest * cap, cap), cap)],
            dst_ref=inbox.at[k, pl.ds(pl.multiple_of(src * cap, cap), cap)],
            send_sem=m_send.at[k, dest], recv_sem=m_recv.at[k, src],
            device_id=(dest, t), device_id_type=MESH,
        )

    share = max(16, (3 * tok // 4) // tensors // 16 * 16)
    zr = share * tensors

    def b_src(dest, row, count):
        return feats.at[dest // bps, pl.ds(row, count), pl.ds(pl.multiple_of(lax.rem(dest, bps) * bw, bw), bw)]

    def b_copy(dest, src):
        return pltpu.make_async_remote_copy(
            src_ref=b_src(dest, zr, tok - zr), dst_ref=blocks.at[src, pl.ds(zr, tok - zr)],
            send_sem=b_send.at[dest], recv_sem=b_recv.at[src],
            device_id=(dest, t), device_id_type=MESH,
        )

    def q_copy(dest, src):
        row = pl.multiple_of(t * share, 16)
        return pltpu.make_async_remote_copy(
            src_ref=b_src(dest, row, share), dst_ref=blocks.at[src, pl.ds(row, share)],
            send_sem=q_send.at[dest], recv_sem=q_recv.at[src],
            device_id=(dest, t), device_id_type=MESH,
        )

    def own_block():
        return pltpu.make_async_copy(b_src(s, zr, tok - zr), blocks.at[s, pl.ds(zr, tok - zr)], b_recv.at[s])

    def own_quarter():
        row = pl.multiple_of(t * share, 16)
        return pltpu.make_async_copy(b_src(s, row, share), blocks.at[s, pl.ds(row, share)], q_recv.at[s])

    def y_copy(way, hop, k, dest):
        rows = pl.ds(pl.multiple_of(k * share, 16), share)
        return pltpu.make_async_remote_copy(
            src_ref=blocks.at[:, rows], dst_ref=blocks.at[:, rows],
            send_sem=y_send.at[way, hop], recv_sem=y_recv.at[way, hop],
            device_id=(s, dest), device_id_type=MESH,
        )

    def y_step(hop):
        for way in range(2):
            k = t - hop if way == 0 else t + hop
            here = k >= 0 if way == 0 else k < tensors
            onward = up_ok if way == 0 else dn_ok
            dest = t + 1 if way == 0 else t - 1

            @pl.when(jnp.logical_and(hop > 0, here))
            def _():
                y_copy(way, hop, k, t).wait_recv()

            @pl.when(jnp.logical_and(here, onward))
            def _():
                y_copy(way, hop + 1, k, dest).start()

    def own_copy(k):
        rows = pl.ds(pl.multiple_of(s * cap, cap), cap)
        return pltpu.make_async_copy(outbox.at[k, rows], inbox.at[k, rows], m_recv.at[k, s])

    def w_copy(weight, buf, which, k):
        return pltpu.make_async_copy(
            weight.at[pl.ds(pl.multiple_of(k * fs, fs), fs)], buf, w_sem.at[which]
        )

    rb = 64

    def scale_rows(read, write, sq, gain, rows):
        def step(i, c):
            rr = pl.ds(pl.multiple_of(i * rb, rb), rb)
            x = read(rr).astype(jnp.float32)
            part = x * x
            total = part[:, 0:128]
            for j in range(1, fs // 128):
                total = total + part[:, j * 128:(j + 1) * 128]
            sq[rr, :] += total
            write(rr, (x * gain).astype(jnp.bfloat16))
            return c
        lax.fori_loop(0, rows // rb, step, 0)

    def accumulate(acc, left, buf):
        def step(n, c):
            cols = pl.ds(pl.multiple_of(n * nt, nt), nt)
            acc[:, cols] += jnp.dot(left[...], buf[:, cols], preferred_element_type=jnp.float32)
            return c
        lax.fori_loop(0, hid // nt, step, 0)

    def arrive(hop):
        for c in range(chunks):
            for way in range(2):
                k = t - hop if way == 0 else t + hop
                here = k >= 0 if way == 0 else k < tensors
                onward = up_ok if way == 0 else dn_ok
                dest = t + 1 if way == 0 else t - 1

                @pl.when(jnp.logical_and(hop > 0, here))
                def _():
                    z_copy(way, hop, c, k, t).wait_recv()

                @pl.when(jnp.logical_and(here, onward))
                def _():
                    z_copy(way, hop + 1, c, k, dest).start()

    def process(k):
        w_copy(weight_a, wbuf_a, 0, k).start()
        pt = min(fs, 256)

        def pack(n, c):
            cols = pl.ds(pl.multiple_of(n * pt, pt), pt)
            outbox[k, :, cols] = jnp.dot(
                dispatch[...], feats[k, :, cols], preferred_element_type=jnp.float32
            ).astype(jnp.bfloat16)
            return c

        lax.fori_loop(0, fs // pt, pack, 0)
        own_copy(k).start()

        def send(r, c):
            m_copy(k, lax.rem(s + r, sections), s).start()
            return c

        lax.fori_loop(1, sections, send, 0)

    def actor(k):
        gain = gain_a[k]

        def write(rr, v):
            work[rr, :] = v

        scale_rows(lambda rr: feats[k, rr, :], write, sq_a, gain, tok)
        w_copy(weight_a, wbuf_a, 0, k).wait()
        accumulate(acc_a, work, wbuf_a)

    def member(k):
        w_copy(weight_m, wbuf_m, 1, k).start()
        own_copy(k).wait()

        def take(r, c):
            m_copy(k, s, lax.rem(s + r, sections)).wait_recv()
            return c

        lax.fori_loop(1, sections, take, 0)
        gain = gain_m[k]

        def write(rr, v):
            inbox[k, rr, :] = v

        scale_rows(lambda rr: inbox[k, rr, :], write, sq_m, gain, slots)
        w_copy(weight_m, wbuf_m, 1, k).wait()
        accumulate(acc_m, inbox.at[k], wbuf_m)

    partner = s + 1 - 2 * lax.rem(s, 2)
    chips = sections // 2
    width = fs * tensors

    def send_block(r, c):
        b_copy(lax.rem(s + r, sections), s).start()
        return c

    def g_copy(dest, src):
        return pltpu.make_async_remote_copy(
            src_ref=early, dst_ref=hidden.at[src],
            send_sem=g_send.at[dest], recv_sem=g_recv.at[src],
            device_id=(dest, t), device_id_type=MESH,
        )

    def g_relay(src):
        return pltpu.make_async_remote_copy(
            src_ref=hidden.at[src], dst_ref=hidden.at[src],
            send_sem=g_pass.at[src], recv_sem=g_recv.at[src],
            device_id=(partner, t), device_id_type=MESH,
        )

    def own_hidden():
        return pltpu.make_async_copy(early, hidden.at[s], g_recv.at[s])

    def t_copy(dest, src):
        return pltpu.make_async_remote_copy(
            src_ref=part.at[src], dst_ref=part.at[src],
            send_sem=t_send.at[dest], recv_sem=t_recv.at[src],
            device_id=(s, dest), device_id_type=MESH,
        )

    def u_copy(dest, src):
        return pltpu.make_async_remote_copy(
            src_ref=part_a.at[src], dst_ref=part_a.at[src],
            send_sem=u_send.at[dest], recv_sem=u_recv.at[src],
            device_id=(s, dest), device_id_type=MESH,
        )

    def r_copy(dest, src):
        return pltpu.make_async_remote_copy(
            src_ref=scores.at[dest], dst_ref=back.at[src],
            send_sem=r_send.at[dest], recv_sem=r_recv.at[src],
            device_id=(dest, t), device_id_type=MESH,
        )

    def p_copy(dest, src):
        return pltpu.make_async_remote_copy(
            src_ref=pairs.at[src], dst_ref=pairs.at[src],
            send_sem=p_send.at[dest], recv_sem=p_recv.at[src],
            device_id=(dest, t), device_id_type=MESH,
        )

    def across(x):
        return lax.dot_general(
            jnp.ones((8, 128), jnp.float32), x, (((1,), (1,)), ((), ())),
            precision=lax.Precision.HIGHEST, preferred_element_type=jnp.float32,
        )

    def fold(x):
        total = x[:, 0:128]
        for j in range(1, hid // 128):
            total = total + x[:, j * 128:(j + 1) * 128]
        return total

    def hidden_step():
        def step(i, c):
            rr = pl.ds(pl.multiple_of(i * rb, rb), rb)
            scale = lax.rsqrt(jnp.sum(sq_a[rr, :], axis=1, keepdims=True) / width + epsilon)
            pre = acc_a[rr, :] * scale
            sig = 1.0 / (1.0 + jnp.exp(-pre))
            row = heads_a[...]
            early[rr, :] = (scale * row * (sig * (1.0 + pre * (1.0 - sig)))).astype(jnp.bfloat16)
            lanes[0, rr, :] = fold(pre * sig * row)
            return c

        lax.fori_loop(0, tok // rb, step, 0)
        part_a[t] = across(lanes[0, 0:tok, :])

        def send_u(r, c):
            u_copy(lax.rem(t + r, tensors), t).start()
            return c

        lax.fori_loop(1, tensors, send_u, 0)
        own_hidden().start()
        g_copy(partner, s).start()

        def send_g(r, c):
            g_copy(lax.rem(s + 2 * r, sections), s).start()
            return c

        lax.fori_loop(1, chips, send_g, 0)

    def score_step():
        def step(i, c):
            rr = pl.ds(pl.multiple_of(i * rb, rb), rb)
            scale = lax.rsqrt(jnp.sum(sq_m[rr, :], axis=1, keepdims=True) / width + epsilon)
            pre = acc_m[rr, :] * scale
            act = pre * (1.0 / (1.0 + jnp.exp(-pre)))
            lanes[0, rr, :] = fold(act * heads_m[0:1, :])
            lanes[1, rr, :] = fold(act * heads_m[1:2, :])
            return c

        lax.fori_loop(0, slots // rb, step, 0)
        first = lax.broadcasted_iota(jnp.int32, (8, cap), 0) == 0

        def gather(d, c):
            rr = pl.ds(pl.multiple_of(d * cap, cap), cap)
            part[t, d] = jnp.where(first, across(lanes[0, rr, :]), across(lanes[1, rr, :]))
            return c

        lax.fori_loop(0, sections, gather, 0)

        def send_t(r, c):
            t_copy(lax.rem(t + r, tensors), t).start()
            return c

        lax.fori_loop(1, tensors, send_t, 0)
        y_step(tensors - 2)

        def take_t(r, c):
            t_copy(t, lax.rem(t + r, tensors)).wait_recv()
            u_copy(t, lax.rem(t + r, tensors)).wait_recv()
            return c

        lax.fori_loop(1, tensors, take_t, 0)
        scores[...] = lax.fori_loop(1, tensors, lambda k, v: v + part[k], part[0])
        shift = lax.fori_loop(1, tensors, lambda k, v: v + part_a[k], part_a[0])

        def send_r(r, c):
            r_copy(lax.rem(s + r, sections), s).start()
            return c

        lax.fori_loop(1, sections, send_r, 0)
        back[s] = scores[s]
        lax.fori_loop(sections - spare, sections, send_block, 0)

        def take_r(r, c):
            r_copy(s, lax.rem(s + r, sections)).wait_recv()
            return c

        lax.fori_loop(1, sections, take_r, 0)

        def pick(m, v):
            x = back[m]
            hi = x.astype(jnp.bfloat16)
            rest = x - hi.astype(jnp.float32)
            mid = rest.astype(jnp.bfloat16)
            low = (rest - mid.astype(jnp.float32)).astype(jnp.bfloat16)
            rows = dispatch[pl.ds(pl.multiple_of(m * cap, cap), cap), :]
            for piece in (low, mid, hi):
                v = v + jnp.dot(piece, rows, preferred_element_type=jnp.float32)
            return v

        picked = lax.fori_loop(0, sections, pick, jnp.zeros((8, tok), jnp.float32))
        values = jnp.broadcast_to(picked[0:1, :], (8, tok))
        rewards = jnp.broadcast_to(picked[1:2, :], (8, tok))
        ended = jnp.broadcast_to(final[...], (8, tok)) > 0.5
        total = jnp.where(ended, rewards, pltpu.roll(values, tok - 1, 1)) - values
        carry = jnp.where(ended, 0.0, trace_decay)
        reach = 1
        while reach < tok:
            total = total + carry * pltpu.roll(total, tok - reach, 1)
            carry = carry * pltpu.roll(carry, tok - reach, 1)
            reach *= 2
        top = lax.broadcasted_iota(jnp.int32, (8, tok), 0) == 0
        pairs[s] = jnp.where(top, total, shift)

        def send_p(r, c):
            p_copy(lax.rem(s + r, sections), s).start()
            return c

        lax.fori_loop(1, sections, send_p, 0)

        def relay(r, c):
            src = lax.rem(s + 2 * r, sections)
            g_copy(s, src).wait_recv()
            g_relay(src).start()
            return c

        lax.fori_loop(1, chips, relay, 0)
        own_hidden().wait()

    def settle():
        g_copy(s, partner).wait_recv()
        g_copy(partner, s).wait_send()

        def done_g(r, c):
            other = lax.rem(s + 2 * r, sections)
            g_copy(other, s).wait_send()
            g_relay(other).wait_send()
            g_copy(s, lax.rem(partner + 2 * r, sections)).wait_recv()
            return c

        lax.fori_loop(1, chips, done_g, 0)

        def done_z(r, c):
            other = lax.rem(t + r, tensors)
            t_copy(other, t).wait_send()
            u_copy(other, t).wait_send()
            return c

        lax.fori_loop(1, tensors, done_z, 0)

        def done_s(r, c):
            other = lax.rem(s + r, sections)
            r_copy(other, s).wait_send()
            p_copy(other, s).wait_send()
            p_copy(s, other).wait_recv()
            return c

        lax.fori_loop(1, sections, done_s, 0)

    spare = max(1, 3 * sections // 8)

    def hop_body(hop, c):
        @pl.when(hop < tensors)
        def _():
            arrive(hop)

        @pl.when(hop == tensors - 1)
        def _():
            own_quarter().start()

            def send(r, c):
                q_copy(lax.rem(s + r, sections), s).start()
                return c

            lax.fori_loop(1, sections, send, 0)

        def inner(way, c):
            k = jnp.where(way == 0, t - hop, t + hop)
            fine = jnp.logical_and(jnp.logical_and(k >= 0, k < tensors), jnp.logical_or(hop > 0, way == 0))
            fine = jnp.logical_and(fine, hop < tensors)

            @pl.when(fine)
            def _():
                process(k)
                actor(k)
            return c

        lax.fori_loop(0, 2, inner, 0)

        @pl.when(hop == tensors - 1)
        def _():
            hidden_step()
            own_block().start()
            lax.fori_loop(1, sections - spare, send_block, 0)
            own_quarter().wait()

            def take(r, c):
                q_copy(s, lax.rem(s + r, sections)).wait_recv()
                return c

            lax.fori_loop(1, sections, take, 0)
            y_step(0)

        @pl.when(hop == tensors)
        def _():
            def onward(h, c):
                y_step(h)
                return c

            lax.fori_loop(1, tensors - 2, onward, 0)

        def inner_m(way, c):
            k = jnp.where(way == 0, t - (hop - 1), t + (hop - 1))
            fine = jnp.logical_and(jnp.logical_and(k >= 0, k < tensors), jnp.logical_or(hop > 1, way == 0))
            fine = jnp.logical_and(fine, hop > 0)

            @pl.when(fine)
            def _():
                member(k)
            return c

        lax.fori_loop(0, 2, inner_m, 0)
        return c

    lax.fori_loop(0, tensors + 1, hop_body, 0)
    score_step()
    settle()

    own_block().wait()
    y_step(tensors - 1)

    def finish(r, c):
        other = lax.rem(s + r, sections)
        b_copy(s, other).wait_recv()
        b_copy(other, s).wait_send()
        q_copy(other, s).wait_send()

        def sent(k, c):
            m_copy(k, other, s).wait_send()
            return c

        return lax.fori_loop(0, tensors, sent, c)

    lax.fori_loop(1, sections, finish, 0)

    def drain(hop, c):
        @pl.when(jnp.logical_and(t - hop >= 0, up_ok))
        def _():
            y_copy(0, hop + 1, t - hop, t + 1).wait_send()

        @pl.when(jnp.logical_and(t + hop < tensors, dn_ok))
        def _():
            y_copy(1, hop + 1, t + hop, t - 1).wait_send()

        for cc in range(chunks):
            @pl.when(jnp.logical_and(t - hop >= 0, up_ok))
            def _():
                z_copy(0, hop + 1, cc, t - hop, t + 1).wait_send()

            @pl.when(jnp.logical_and(t + hop < tensors, dn_ok))
            def _():
                z_copy(1, hop + 1, cc, t + hop, t - 1).wait_send()
        return c

    lax.fori_loop(0, tensors, drain, 0)


def body(
    states, lengths, routes, score_gain, score_weight, score_heads,
    actor_gain, actor_weight, actor_heads,
):
    sections = lax.axis_size("section")
    tensors = lax.axis_size("tensor")
    tok, fs = states.shape
    cap = 2 * tok // sections
    slots = sections * cap
    width = score_gain.shape[1]
    hid = actor_weight.shape[1]
    bw = width // sections
    target = routes[:, 0]
    ids = jnp.arange(tok, dtype=jnp.int32)
    same = jnp.logical_and(target[:, None] == target[None, :], ids[:, None] > ids[None, :])
    placed = jnp.sum(same.astype(jnp.int32), axis=1)
    slot_index = target * cap + placed
    hit = jnp.arange(slots, dtype=jnp.int32)[:, None] == slot_index[None, :]
    dispatch = hit.astype(jnp.bfloat16)
    count = lengths.shape[1]
    order = jnp.arange(count, dtype=jnp.int32)
    ends = jnp.sum(jnp.where(order[:, None] <= order[None, :], lengths[0][:, None], 0), axis=0) - 1
    last = jnp.any(ends[:, None] == ids[None, :], axis=0)

    vmem = pl.BlockSpec(memory_space=pltpu.VMEM)
    any_ = pl.BlockSpec(memory_space=pl.ANY)
    f32, bf16 = jnp.float32, jnp.bfloat16
    scores, pairs, blocks, hidden = pl.pallas_call(
        functools.partial(exchange, sections, tensors, cap),
        out_shape=(
            jax.ShapeDtypeStruct((sections, 8, cap), f32),
            jax.ShapeDtypeStruct((sections, 8, tok), f32),
            jax.ShapeDtypeStruct((sections, tok, bw), bf16),
            jax.ShapeDtypeStruct((sections, tok, hid), bf16),
        ),
        in_specs=[any_, vmem, vmem, vmem, any_, any_, vmem, vmem, vmem],
        out_specs=(vmem, vmem, any_, any_),
        scratch_shapes=[
            pltpu.VMEM((slots, hid), f32),
            pltpu.VMEM((tok, hid), f32),
            pltpu.VMEM((slots, 128), f32),
            pltpu.VMEM((tok, 128), f32),
            pltpu.VMEM((2, max(slots, tok), 128), f32),
            pltpu.VMEM((tensors, sections, 8, cap), f32),
            pltpu.VMEM((tensors, 8, tok), f32),
            pltpu.VMEM((sections, 8, cap), f32),
            pltpu.VMEM((tok, hid), bf16),
            pltpu.VMEM((tensors, tok, fs), bf16),
            pltpu.VMEM((tensors, slots, fs), bf16),
            pltpu.VMEM((tensors, slots, fs), bf16),
            pltpu.VMEM((tok, fs), bf16),
            pltpu.VMEM((fs, hid), bf16),
            pltpu.VMEM((fs, hid), bf16),
            pltpu.SemaphoreType.DMA((2, tensors + 1, 2)),
            pltpu.SemaphoreType.DMA((2, tensors + 1, 2)),
            pltpu.SemaphoreType.DMA((tensors, sections)),
            pltpu.SemaphoreType.DMA((tensors, sections)),
            pltpu.SemaphoreType.DMA((sections,)),
            pltpu.SemaphoreType.DMA((sections,)),
            pltpu.SemaphoreType.DMA((1,)),
            pltpu.SemaphoreType.DMA((2,)),
            pltpu.SemaphoreType.DMA((tensors,)),
            pltpu.SemaphoreType.DMA((tensors,)),
            pltpu.SemaphoreType.DMA((tensors,)),
            pltpu.SemaphoreType.DMA((tensors,)),
            pltpu.SemaphoreType.DMA((sections,)),
            pltpu.SemaphoreType.DMA((sections,)),
            pltpu.SemaphoreType.DMA((sections,)),
            pltpu.SemaphoreType.DMA((sections,)),
            pltpu.SemaphoreType.DMA((sections,)),
            pltpu.SemaphoreType.DMA((sections,)),
            pltpu.SemaphoreType.DMA((sections,)),
            pltpu.SemaphoreType.DMA((sections,)),
            pltpu.SemaphoreType.DMA((sections,)),
            pltpu.SemaphoreType.DMA((2, tensors + 1)),
            pltpu.SemaphoreType.DMA((2, tensors + 1)),
        ],
        compiler_params=pltpu.CompilerParams(
            collective_id=0, has_side_effects=True, vmem_limit_bytes=67043328
        ),
    )(
        states, dispatch, score_gain[0].reshape(tensors, 1, fs),
        actor_gain.reshape(tensors, 1, fs), score_weight[0], actor_weight,
        jnp.transpose(score_heads[0]), actor_heads[None, :], last.astype(f32)[None, :],
    )

    raw_all = pairs[:, 0].reshape(-1)
    shift_all = pairs[:, 1].reshape(-1)
    raw = lax.dynamic_index_in_dim(pairs, lax.axis_index("section"), 0, keepdims=False)[0]
    total = tok * sections
    center = jnp.sum(raw_all) / total
    spread = jnp.sum(raw_all * raw_all) / total - center * center
    inv = lax.rsqrt(spread + epsilon)
    advantages = (raw - center) * inv
    ratios = jnp.exp(shift_all)
    slope = penalty * (ratios - 1.0) - ratios * ((raw_all - center) * inv)

    gain_own = lax.dynamic_slice(actor_gain, (lax.axis_index("section") * bw,), (bw,))
    left = (blocks.reshape(total, bw).astype(f32) * gain_own[None, :]).astype(bf16)
    right = (hidden.reshape(total, hid).astype(f32) * slope[:, None]).astype(bf16)
    actor_grad = lax.dot_general(
        left, right, (((0,), (0,)), ((), ())), preferred_element_type=f32
    )
    packed_scores = jnp.transpose(scores[:, :2], (1, 0, 2)).reshape(2, slots)
    return (packed_scores, advantages, actor_grad)


def solution(mesh):
    in_specs = (
        P("section", "tensor"),
        P("section", None),
        P("section", None),
        P("section", None),
        P("section", None, "tensor"),
        P("section", "tensor", None),
        P(),
        P(None, "tensor"),
        P("tensor"),
    )
    out_specs = (P(None, "section"), P("section"), P("section", "tensor"))
    return jax.shard_map(body, mesh=mesh, in_specs=in_specs, out_specs=out_specs, check_vma=False)
```
